256 devices in a mesh: gx: 8 (over y, core), gy: 32 (over x, z).
Axes of the slice: x: 4, y: 4, z: 8, core: 2. Of those that a mesh axis runs over, the one named last changes fastest.
Arguments:
- features: bfloat16 [8, 32, 2, 512, 128], P('gx', 'gy'), may hold values from -6 to 6
- grad_out: bfloat16 [8, 32, 2, 512, 128], P('gx', 'gy'), may hold values from -6 to 6
- weight: bfloat16 [27, 128, 128], replicated, may hold values from -0.109375 to 0.109375
- neighbours: int32 [8, 32, 2, 27], P('gx', 'gy'), may hold values from -1 to 17, as said below
Outputs:
- out_features: bfloat16 [8, 32, 2, 512, 128], P('gx', 'gy')
- grad_features: bfloat16 [8, 32, 2, 512, 128], P('gx', 'gy')
- grad_weight: float32 [27, 128, 128], replicated
The draws below stay inside these ranges and needn't reach their ends.
Inputs may be any that keep to these rules, and one draw needn't show every extreme that they name: neighbours[i, j, s, k] is (3 * (di + 1) + (dj + 1)) * 2 + t when the block at offset k from slot s of region (i, j) is active and sits in slot t of region (i + di, j + dj), with di and dj in -1, 0, 1; else -1. Blocks lie on a scene of 16 x 64 x 1 positions, region (i, j) owning x positions 2i, 2i + 1 and y positions 2j, 2j + 1; the relation is symmetric. Each region has 1 to 2 active slots, its first ones, and some region has all 2; an inactive slot has -1 in every entry and its features and grad_out are never read.
All inputs are finite; a program needn't handle non-finite values.
Results may differ from the reference program's by a relative error of at most 0.001.
Values may be sent and summed in bfloat16 or wider, within the bound.
A program may use at most 64 MiB of HBM per device.

```python
import math
import jax
import jax.numpy as jnp
from jax import lax

C = 128
BLK = 8
B_DEV = 2
VOX = 512
DEPTH = 1
GRID_X = 16
GRID_Y = 64
N_GX = 8
N_GY = 32


def draw_neighbours(key, part):
    regions_x = GRID_X // 2
    regions_y = GRID_Y // 2
    region_total = regions_x * regions_y
    places = 4 * DEPTH
    counts = jax.random.randint(jax.random.fold_in(key, 11), (region_total,), B_DEV // 2, B_DEV + 1)
    fullest = jax.random.randint(jax.random.fold_in(key, 12), (), 0, region_total)
    counts = jnp.where(jnp.arange(region_total) == fullest, B_DEV, counts).astype(jnp.int32)
    region_keys = jax.random.split(jax.random.fold_in(key, 13), region_total)
    orders = jax.vmap(lambda k: jax.random.permutation(k, places))(region_keys).astype(jnp.int32)
    inverse = jnp.argsort(orders, axis=1).astype(jnp.int32)
    slot_grid = jnp.where(inverse < counts[:, None], inverse, -1)
    slot_grid = slot_grid.reshape(regions_x, regions_y, 2, 2, DEPTH).transpose(0, 2, 1, 3, 4).reshape(GRID_X, GRID_Y, DEPTH)
    chosen = orders[:, :B_DEV]
    region_ids = jnp.arange(region_total, dtype=jnp.int32)
    row_of = (region_ids // regions_y)[:, None]
    col_of = (region_ids % regions_y)[:, None]
    active = jnp.arange(B_DEV, dtype=jnp.int32)[None, :] < counts[:, None]
    place_x = row_of * 2 + chosen // (2 * DEPTH)
    place_y = col_of * 2 + chosen // DEPTH % 2
    place_z = chosen % DEPTH
    entries = []
    for a in range(3):
        for b in range(3):
            for c in range(3):
                target_x = place_x + (a - 1)
                target_y = place_y + (b - 1)
                target_z = place_z + (c - 1)
                inside = (target_x >= 0) & (target_x < GRID_X) & (target_y >= 0) & (target_y < GRID_Y) & (target_z >= 0) & (target_z < DEPTH)
                target = slot_grid[jnp.clip(target_x, 0, GRID_X - 1), jnp.clip(target_y, 0, GRID_Y - 1), jnp.clip(target_z, 0, DEPTH - 1)]
                region_code = (target_x // 2 - row_of + 1) * 3 + (target_y // 2 - col_of + 1)
                encoded = region_code * B_DEV + target
                entries.append(jnp.where(active & inside & (target >= 0), encoded, -1))
    result = jnp.stack(entries, axis=-1).reshape(regions_x, regions_y, B_DEV, 27)
    return result.astype(jnp.int32)


def block_scale(own_key, dims, pieces, smallest, largest):
    loudness = 1.0
    for axis_at, blocks in pieces:
        heights = jax.random.uniform(jax.random.fold_in(jax.random.fold_in(own_key, 6), axis_at), (blocks,), jnp.float32, smallest / len(pieces), largest / len(pieces))
        loudness = loudness * jnp.repeat(jnp.exp(heights), dims[axis_at] // blocks).reshape((-1,) + (1,) * (len(dims) - 1 - axis_at))
    return loudness


def centred(key, dims, deviation, bound, cuts=(), kind=jnp.bfloat16):
    values = jax.random.normal(key, dims, jnp.float32) * deviation
    if len(cuts) > 0:
        values = block_scale(key, dims, cuts, -0.22, 0.18) * values
    return jnp.clip(values, min=-bound, max=bound).astype(kind)


def setup_inputs(seed: int = 0) -> dict:
    streams_of = jax.random.split(jax.random.key(seed), 5)
    features = centred(streams_of[0], (N_GX, N_GY, B_DEV, VOX, C), 1.0, 6.0, ((0, 8), (1, 32)))
    grad_out = centred(streams_of[1], (N_GX, N_GY, B_DEV, VOX, C), 1.0, 6.0, ((0, 8), (1, 32)))
    weight = centred(streams_of[2], (27, C, C), (27 * C) ** -0.5, 0.109375)
    neighbours = draw_neighbours(jax.random.fold_in(streams_of[4], 71), 0)
    return {"features": features, "grad_out": grad_out, "weight": weight, "neighbours": neighbours}


def assemble(block_pool, neighbour_ids, block_edge):
    slot_count = neighbour_ids.shape[0]
    channels = block_pool.shape[-1]
    ranges = ((block_edge - 1, block_edge), (0, block_edge), (0, 1))
    planes = []
    for a in range(3):
        row_list = []
        for b in range(3):
            columns = []
            for c in range(3):
                chosen_ids = neighbour_ids[:, (a * 3 + b) * 3 + c]
                picked = jnp.take(block_pool, jnp.maximum(chosen_ids, 0), axis=0)
                picked = jnp.where((chosen_ids >= 0)[:, None, None], picked, jnp.zeros((), block_pool.dtype))
                portion = picked.reshape(slot_count, block_edge, block_edge, block_edge, channels)
                portion = portion[:, ranges[a][0]:ranges[a][1], ranges[b][0]:ranges[b][1], ranges[c][0]:ranges[c][1], :]
                columns.append(portion)
            row_list.append(jnp.concatenate(columns, axis=3))
        planes.append(jnp.concatenate(row_list, axis=2))
    return jnp.concatenate(planes, axis=1)

def local_pass(pool_feat, pool_grad, own_grad, neighbour_ids, weight, block_edge):
    channels = weight.shape[-1]
    padded_feat = assemble(pool_feat, neighbour_ids, block_edge)
    padded_grad = assemble(pool_grad, neighbour_ids, block_edge)
    grad_flat = own_grad.reshape(-1, channels)
    running_out = None
    running_in = None
    partial_value = []
    for a in range(3):
        for b in range(3):
            for c in range(3):
                k = (a * 3 + b) * 3 + c
                window = padded_feat[:, a:a + block_edge, b:b + block_edge, c:c + block_edge, :].reshape(-1, channels)
                term_out = jnp.dot(window, weight[k], preferred_element_type=jnp.float32)
                running_out = term_out if running_out is None else running_out + term_out
                partial_value.append(lax.dot_general(window, grad_flat, (((0,), (0,)), ((), ())), preferred_element_type=jnp.float32))
                back_window = padded_grad[:, 2 - a:2 - a + block_edge, 2 - b:2 - b + block_edge, 2 - c:2 - c + block_edge, :].reshape(-1, channels)
                term_in = lax.dot_general(back_window, weight[k], (((1,), (1,)), ((), ())), preferred_element_type=jnp.float32)
                running_in = term_in if running_in is None else running_in + term_in
    return (running_out.astype(jnp.bfloat16), running_in.astype(jnp.bfloat16), jnp.stack(partial_value))

def reference(features, grad_out, weight, neighbours):
    widths = ((1, 1), (1, 1), (0, 0), (0, 0), (0, 0))
    feat_padded = jnp.pad(features, widths)
    grad_padded = jnp.pad(grad_out, widths)
    slot_count = features.shape[2]
    voxels = features.shape[3]
    channels = features.shape[4]

    def one_region(carry, region):
        row_at = (region // N_GY).astype(jnp.int32)
        col_at = (region % N_GY).astype(jnp.int32)
        zero = jnp.int32(0)
        anchor = (row_at, col_at, zero, zero, zero)
        sizes_cut = (3, 3, slot_count, voxels, channels)
        pool_feat = lax.dynamic_slice(feat_padded, anchor, sizes_cut).reshape(9 * slot_count, voxels, channels)
        pool_grad = lax.dynamic_slice(grad_padded, anchor, sizes_cut).reshape(9 * slot_count, voxels, channels)
        own_grad = lax.dynamic_slice(grad_out, (row_at, col_at, zero, zero, zero), (1, 1, slot_count, voxels, channels))
        neighbour_ids = lax.dynamic_slice(neighbours, (row_at, col_at, zero, zero), (1, 1, slot_count, 27)).reshape(slot_count, 27)
        output, grad_in, partial_value = local_pass(pool_feat, pool_grad, own_grad, neighbour_ids, weight, BLK)
        return (carry + partial_value, (output, grad_in))
    start = jnp.zeros((27, channels, channels), jnp.float32)
    summed, (outputs, grads_in) = lax.scan(one_region, start, jnp.arange(N_GX * N_GY, dtype=jnp.int32))
    scale_factor = 1.0 / math.sqrt(N_GX * N_GY * slot_count * voxels)
    return (outputs.reshape(features.shape), grads_in.reshape(features.shape), summed * scale_factor)
```

```python
import math

import jax
import jax.numpy as jnp
from jax import lax
from jax.sharding import PartitionSpec as P

BLK = 8


def shift(x, axes, step):
    sizes = [lax.axis_size(a) for a in axes]
    pairs = []
    for src in range(math.prod(sizes)):
        coords, rest = [], src
        for size in reversed(sizes):
            coords.append(rest % size)
            rest //= size
        coords = coords[::-1]
        dst = [c + d for c, d in zip(coords, step)]
        if all(0 <= c < s for c, s in zip(dst, sizes)):
            flat = 0
            for c, s in zip(dst, sizes):
                flat = flat * s + c
            pairs.append((src, flat))
    return lax.ppermute(x, axes if len(axes) > 1 else axes[0], pairs)


def neighbour_pool(both):
    x7, x0 = both[:, :, 7], both[:, :, 0]
    y7, y0 = both[:, :, :, 7], both[:, :, :, 0]
    zero = jnp.zeros_like(both)
    recv = {
        (-1, 0): zero.at[:, :, 7].set(shift(x7, ("gx",), (1,))),
        (1, 0): zero.at[:, :, 0].set(shift(x0, ("gx",), (-1,))),
        (0, -1): zero.at[:, :, :, 7].set(shift(y7, ("gy",), (1,))),
        (0, 1): zero.at[:, :, :, 0].set(shift(y0, ("gy",), (-1,))),
        (-1, -1): zero.at[:, :, 7, 7].set(shift(both[:, :, 7, 7], ("gx", "gy"), (1, 1))),
        (-1, 1): zero.at[:, :, 7, 0].set(shift(both[:, :, 7, 0], ("gx", "gy"), (1, -1))),
        (1, -1): zero.at[:, :, 0, 7].set(shift(both[:, :, 0, 7], ("gx", "gy"), (-1, 1))),
        (1, 1): zero.at[:, :, 0, 0].set(shift(both[:, :, 0, 0], ("gx", "gy"), (-1, -1))),
        (0, 0): both,
    }
    blocks = [recv[(di, dj)] for di in (-1, 0, 1) for dj in (-1, 0, 1)]
    pool = jnp.stack(blocks, axis=1)
    return pool.reshape(2, 9 * both.shape[1], -1)


def assemble(picked, block_edge):
    ranges = ((block_edge - 1, block_edge), (0, block_edge), (0, 1))
    planes = []
    for a in range(3):
        row_list = []
        for b in range(3):
            columns = []
            for c in range(3):
                k = (a * 3 + b) * 3 + c
                portion = picked[
                    :,
                    k,
                    :,
                    ranges[a][0] : ranges[a][1],
                    ranges[b][0] : ranges[b][1],
                    ranges[c][0] : ranges[c][1],
                    :,
                ]
                columns.append(portion)
            row_list.append(jnp.concatenate(columns, axis=4))
        planes.append(jnp.concatenate(row_list, axis=3))
    cube = jnp.concatenate(planes, axis=2)
    return jnp.swapaxes(cube, 0, 1)


def im2col(cube, block_edge):
    windows = []
    for a in range(3):
        for b in range(3):
            for c in range(3):
                windows.append(
                    cube[:, a : a + block_edge, b : b + block_edge, c : c + block_edge, :]
                )
    cols = jnp.concatenate(windows, axis=-1)
    return cols.reshape(-1, cols.shape[-1])


def butterfly_sum(x, axes):
    n = math.prod(lax.axis_size(a) for a in axes)
    bits = n.bit_length() - 1
    flat = x.reshape(-1)
    me = lax.axis_index(axes)
    gx_bits = int(math.log2(lax.axis_size(axes[0])))
    gy_bits = bits - gx_bits
    order = [gy_bits + i for i in range(gx_bits)] + list(range(gy_bits))
    order = [order[0]] + sorted(order[1:], key=lambda b: (b % 3, b))
    pairs = lambda b: [(j, j ^ (1 << b)) for j in range(n)]
    for b in order:
        half = flat.shape[0] // 2
        bit = (me >> b) & 1
        keep = lax.dynamic_slice(flat, (bit * half,), (half,))
        send = lax.dynamic_slice(flat, ((1 - bit) * half,), (half,))
        flat = keep + lax.ppermute(send, axes, pairs(b))
    for b in reversed(order):
        bit = (me >> b) & 1
        other = lax.ppermute(flat, axes, pairs(b))
        flat = jnp.where(
            bit == 0, jnp.concatenate([flat, other]), jnp.concatenate([other, flat])
        )
    return flat.reshape(x.shape)


def local(features, grad_out, weight, neighbours):
    slot_count = features.shape[2]
    voxels = features.shape[3]
    channels = features.shape[4]
    e = BLK
    both = jnp.stack([features[0, 0], grad_out[0, 0]]).reshape(
        2, slot_count, e, e, e, channels
    )
    pool = neighbour_pool(both)
    ids = neighbours.reshape(slot_count * 27)
    onehot = (ids[:, None] == jnp.arange(pool.shape[1])[None, :]).astype(pool.dtype)
    picked = jnp.einsum(
        "mn,anf->maf", onehot, pool, preferred_element_type=jnp.float32
    ).astype(pool.dtype)
    picked = picked.reshape(slot_count, 27, 2, e, e, e, channels)
    cubes = assemble(picked, e)
    cols_feat = im2col(cubes[0], e)
    cols_grad = im2col(cubes[1], e)
    grad_flat = grad_out.reshape(-1, channels)
    partial_value = lax.dot_general(
        cols_feat, grad_flat, (((0,), (0,)), ((), ())), preferred_element_type=jnp.float32
    ).reshape(27, channels, channels)
    summed = butterfly_sum(partial_value, ("gx", "gy"))
    w_out = weight.reshape(27 * channels, channels)
    w_in = jnp.swapaxes(weight[::-1], 1, 2).reshape(27 * channels, channels)
    output = jnp.dot(cols_feat, w_out, preferred_element_type=jnp.float32)
    grad_in = jnp.dot(cols_grad, w_in, preferred_element_type=jnp.float32)
    total_slots = lax.axis_size("gx") * lax.axis_size("gy") * slot_count * voxels
    scale_factor = 1.0 / math.sqrt(total_slots)
    return (
        output.astype(jnp.bfloat16).reshape(features.shape),
        grad_in.astype(jnp.bfloat16).reshape(features.shape),
        summed * scale_factor,
    )


def solution(mesh):
    in_specs = (
        P("gx", "gy", None, None, None),
        P("gx", "gy", None, None, None),
        P(),
        P("gx", "gy", None, None),
    )
    out_specs = (P("gx", "gy", None, None, None), P("gx", "gy", None, None, None), P())
    return jax.shard_map(local, mesh=mesh, in_specs=in_specs, out_specs=out_specs, check_vma=False)
```

```python
import math

import jax
import jax.numpy as jnp
from jax import lax
from jax.sharding import PartitionSpec as P

BLK = 8


def shift(x, axes, step):
    sizes = [lax.axis_size(a) for a in axes]
    pairs = []
    for src in range(math.prod(sizes)):
        coords, rest = [], src
        for size in reversed(sizes):
            coords.append(rest % size)
            rest //= size
        coords = coords[::-1]
        dst = [c + d for c, d in zip(coords, step)]
        if all(0 <= c < s for c, s in zip(dst, sizes)):
            flat = 0
            for c, s in zip(dst, sizes):
                flat = flat * s + c
            pairs.append((src, flat))
    return lax.ppermute(x, axes if len(axes) > 1 else axes[0], pairs)


def neighbour_pool(blocks, block_edge):
    e = block_edge
    s, v, c = blocks.shape
    rows = blocks.reshape(s, e, e * e, c)
    hi, lo = (e - 1) * e, e
    zero = jnp.zeros_like(rows)
    recv = {
        (-1, 0): zero.at[:, e - 1].set(shift(rows[:, e - 1], ("gx",), (1,))),
        (1, 0): zero.at[:, 0].set(shift(rows[:, 0], ("gx",), (-1,))),
        (0, -1): zero.at[:, :, hi:].set(shift(rows[:, :, hi:], ("gy",), (1,))),
        (0, 1): zero.at[:, :, :lo].set(shift(rows[:, :, :lo], ("gy",), (-1,))),
        (-1, -1): zero.at[:, e - 1, hi:].set(shift(rows[:, e - 1, hi:], ("gx", "gy"), (1, 1))),
        (-1, 1): zero.at[:, e - 1, :lo].set(shift(rows[:, e - 1, :lo], ("gx", "gy"), (1, -1))),
        (1, -1): zero.at[:, 0, hi:].set(shift(rows[:, 0, hi:], ("gx", "gy"), (-1, 1))),
        (1, 1): zero.at[:, 0, :lo].set(shift(rows[:, 0, :lo], ("gx", "gy"), (-1, -1))),
        (0, 0): rows,
    }
    pool = jnp.concatenate([recv[(di, dj)] for di in (-1, 0, 1) for dj in (-1, 0, 1)])
    return pool.reshape(9 * s, v, c)


def padded_columns(blocks, ids, block_edge):
    e = block_edge
    s, v, c = blocks.shape
    pool = neighbour_pool(blocks, e)
    onehot = (ids[:, None] == jnp.arange(pool.shape[0])[None, :]).astype(pool.dtype)
    picked = jnp.einsum("mn,nvc->mvc", onehot, pool, preferred_element_type=jnp.float32)
    picked = picked.reshape(s, 27, e, e, e, c)
    cube = assemble(picked, e)
    return im2col(cube, e).astype(blocks.dtype)


def assemble(picked, block_edge):
    ranges = ((block_edge - 1, block_edge), (0, block_edge), (0, 1))
    planes = []
    for a in range(3):
        row_list = []
        for b in range(3):
            columns = []
            for c in range(3):
                k = (a * 3 + b) * 3 + c
                portion = picked[
                    :,
                    k,
                    ranges[a][0] : ranges[a][1],
                    ranges[b][0] : ranges[b][1],
                    ranges[c][0] : ranges[c][1],
                    :,
                ]
                columns.append(portion)
            row_list.append(jnp.concatenate(columns, axis=3))
        planes.append(jnp.concatenate(row_list, axis=2))
    return jnp.concatenate(planes, axis=1)


def im2col(cube, block_edge):
    windows = []
    for a in range(3):
        for b in range(3):
            for c in range(3):
                windows.append(
                    cube[:, a : a + block_edge, b : b + block_edge, c : c + block_edge, :]
                )
    cols = jnp.concatenate(windows, axis=-1)
    return cols.reshape(-1, cols.shape[-1])


def butterfly_sum(x, axes):
    n = math.prod(lax.axis_size(a) for a in axes)
    bits = n.bit_length() - 1
    flat = x.reshape(-1)
    me = lax.axis_index(axes)
    gx_bits = int(math.log2(lax.axis_size(axes[0])))
    gy_bits = bits - gx_bits
    order = [gy_bits + i for i in range(gx_bits)] + list(range(gy_bits))
    order = [order[0]] + sorted(order[1:], key=lambda b: (b % 3, b))
    pairs = lambda b: [(j, j ^ (1 << b)) for j in range(n)]
    for b in order:
        half = flat.shape[0] // 2
        bit = (me >> b) & 1
        keep = lax.dynamic_slice(flat, (bit * half,), (half,))
        send = lax.dynamic_slice(flat, ((1 - bit) * half,), (half,))
        flat = keep + lax.ppermute(send, axes, pairs(b))
    for b in reversed(order):
        bit = (me >> b) & 1
        other = lax.ppermute(flat, axes, pairs(b))
        flat = jnp.where(
            bit == 0, jnp.concatenate([flat, other]), jnp.concatenate([other, flat])
        )
    return flat.reshape(x.shape)


def local(features, grad_out, weight, neighbours):
    slot_count = features.shape[2]
    voxels = features.shape[3]
    channels = features.shape[4]
    ids = neighbours.reshape(slot_count * 27)
    cols_feat = padded_columns(features.reshape(slot_count, voxels, channels), ids, BLK)
    grad_flat = grad_out.reshape(-1, channels)
    partial_value = lax.dot_general(
        cols_feat, grad_flat, (((0,), (0,)), ((), ())), preferred_element_type=jnp.float32
    ).reshape(27, channels, channels)
    summed = butterfly_sum(partial_value, ("gx", "gy"))
    cols_grad = padded_columns(grad_out.reshape(slot_count, voxels, channels), ids, BLK)
    w_out = weight.reshape(27 * channels, channels)
    w_in = jnp.swapaxes(weight[::-1], 1, 2).reshape(27 * channels, channels)
    output = jnp.dot(cols_feat, w_out, preferred_element_type=jnp.float32)
    grad_in = jnp.dot(cols_grad, w_in, preferred_element_type=jnp.float32)
    total_slots = lax.axis_size("gx") * lax.axis_size("gy") * slot_count * voxels
    scale_factor = 1.0 / math.sqrt(total_slots)
    return (
        output.astype(jnp.bfloat16).reshape(features.shape),
        grad_in.astype(jnp.bfloat16).reshape(features.shape),
        summed * scale_factor,
    )


def solution(mesh):
    in_specs = (
        P("gx", "gy", None, None, None),
        P("gx", "gy", None, None, None),
        P(),
        P("gx", "gy", None, None),
    )
    out_specs = (P("gx", "gy", None, None, None), P("gx", "gy", None, None, None), P())
    return jax.shard_map(local, mesh=mesh, in_specs=in_specs, out_specs=out_specs, check_vma=False)
```

```python
import math

import jax
import jax.numpy as jnp
from jax import lax
from jax.sharding import PartitionSpec as P

BLK = 8


def shift(x, axes, step):
    sizes = [lax.axis_size(a) for a in axes]
    pairs = []
    for src in range(math.prod(sizes)):
        coords, rest = [], src
        for size in reversed(sizes):
            coords.append(rest % size)
            rest //= size
        coords = coords[::-1]
        dst = [c + d for c, d in zip(coords, step)]
        if all(0 <= c < s for c, s in zip(dst, sizes)):
            flat = 0
            for c, s in zip(dst, sizes):
                flat = flat * s + c
            pairs.append((src, flat))
    return lax.ppermute(x, axes if len(axes) > 1 else axes[0], pairs)


def neighbour_pool(blocks, block_edge):
    e = block_edge
    n, s, v, c = blocks.shape
    rows = blocks.reshape(n, s, e, e * e, c)
    hi, lo = (e - 1) * e, e
    zero = jnp.zeros_like(rows)
    recv = {
        (-1, 0): zero.at[:, :, e - 1].set(shift(rows[:, :, e - 1], ("gx",), (1,))),
        (1, 0): zero.at[:, :, 0].set(shift(rows[:, :, 0], ("gx",), (-1,))),
        (0, -1): zero.at[:, :, :, hi:].set(shift(rows[:, :, :, hi:], ("gy",), (1,))),
        (0, 1): zero.at[:, :, :, :lo].set(shift(rows[:, :, :, :lo], ("gy",), (-1,))),
        (-1, -1): zero.at[:, :, e - 1, hi:].set(
            shift(rows[:, :, e - 1, hi:], ("gx", "gy"), (1, 1))
        ),
        (-1, 1): zero.at[:, :, e - 1, :lo].set(
            shift(rows[:, :, e - 1, :lo], ("gx", "gy"), (1, -1))
        ),
        (1, -1): zero.at[:, :, 0, hi:].set(shift(rows[:, :, 0, hi:], ("gx", "gy"), (-1, 1))),
        (1, 1): zero.at[:, :, 0, :lo].set(shift(rows[:, :, 0, :lo], ("gx", "gy"), (-1, -1))),
        (0, 0): rows,
    }
    pool = jnp.concatenate(
        [recv[(di, dj)] for di in (-1, 0, 1) for dj in (-1, 0, 1)], axis=1
    )
    return pool.reshape(n, 9 * s, v, c)


def padded_columns(pool, ids, slot_count, block_edge):
    e = block_edge
    c = pool.shape[-1]
    onehot = (ids[:, None] == jnp.arange(pool.shape[0])[None, :]).astype(pool.dtype)
    picked = jnp.einsum("mn,nvc->mvc", onehot, pool, preferred_element_type=jnp.float32)
    picked = picked.reshape(slot_count, 27, e, e, e, c)
    cube = assemble(picked, e)
    return im2col(cube, e).astype(pool.dtype)


def assemble(picked, block_edge):
    ranges = ((block_edge - 1, block_edge), (0, block_edge), (0, 1))
    planes = []
    for a in range(3):
        row_list = []
        for b in range(3):
            columns = []
            for c in range(3):
                k = (a * 3 + b) * 3 + c
                portion = picked[
                    :,
                    k,
                    ranges[a][0] : ranges[a][1],
                    ranges[b][0] : ranges[b][1],
                    ranges[c][0] : ranges[c][1],
                    :,
                ]
                columns.append(portion)
            row_list.append(jnp.concatenate(columns, axis=3))
        planes.append(jnp.concatenate(row_list, axis=2))
    return jnp.concatenate(planes, axis=1)


def im2col(cube, block_edge):
    windows = []
    for a in range(3):
        for b in range(3):
            for c in range(3):
                windows.append(
                    cube[:, a : a + block_edge, b : b + block_edge, c : c + block_edge, :]
                )
    cols = jnp.concatenate(windows, axis=-1)
    return cols.reshape(-1, cols.shape[-1])


def butterfly_sum(x, axes):
    n = math.prod(lax.axis_size(a) for a in axes)
    bits = n.bit_length() - 1
    flat = x.reshape(-1)
    me = lax.axis_index(axes)
    gx_bits = int(math.log2(lax.axis_size(axes[0])))
    gy_bits = bits - gx_bits
    order = [gy_bits + i for i in range(gx_bits)] + list(range(gy_bits))
    order = [order[0]] + sorted(order[1:], key=lambda b: (b % 3, b))
    pairs = lambda b: [(j, j ^ (1 << b)) for j in range(n)]
    for b in order:
        half = flat.shape[0] // 2
        bit = (me >> b) & 1
        keep = lax.dynamic_slice(flat, (bit * half,), (half,))
        send = lax.dynamic_slice(flat, ((1 - bit) * half,), (half,))
        flat = keep + lax.ppermute(send, axes, pairs(b))
    for b in reversed(order):
        bit = (me >> b) & 1
        other = lax.ppermute(flat, axes, pairs(b))
        flat = jnp.where(
            bit == 0, jnp.concatenate([flat, other]), jnp.concatenate([other, flat])
        )
    return flat.reshape(x.shape)


def local(features, grad_out, weight, neighbours):
    slot_count = features.shape[2]
    voxels = features.shape[3]
    channels = features.shape[4]
    ids = neighbours.reshape(slot_count * 27)
    both = jnp.stack([features, grad_out]).reshape(2, slot_count, voxels, channels)
    pool = neighbour_pool(both, BLK)
    cols_feat = padded_columns(pool[0], ids, slot_count, BLK)
    grad_flat = grad_out.reshape(-1, channels)
    partial_value = lax.dot_general(
        cols_feat, grad_flat, (((0,), (0,)), ((), ())), preferred_element_type=jnp.float32
    ).reshape(27, channels, channels)
    summed = butterfly_sum(partial_value, ("gx", "gy"))
    cols_grad = padded_columns(pool[1], ids, slot_count, BLK)
    w_out = weight.reshape(27 * channels, channels)
    w_in = jnp.swapaxes(weight[::-1], 1, 2).reshape(27 * channels, channels)
    output = jnp.dot(cols_feat, w_out, preferred_element_type=jnp.float32)
    grad_in = jnp.dot(cols_grad, w_in, preferred_element_type=jnp.float32)
    total_slots = lax.axis_size("gx") * lax.axis_size("gy") * slot_count * voxels
    scale_factor = 1.0 / math.sqrt(total_slots)
    return (
        output.astype(jnp.bfloat16).reshape(features.shape),
        grad_in.astype(jnp.bfloat16).reshape(features.shape),
        summed * scale_factor,
    )


def solution(mesh):
    in_specs = (
        P("gx", "gy", None, None, None),
        P("gx", "gy", None, None, None),
        P(),
        P("gx", "gy", None, None),
    )
    out_specs = (P("gx", "gy", None, None, None), P("gx", "gy", None, None, None), P())
    return jax.shard_map(local, mesh=mesh, in_specs=in_specs, out_specs=out_specs, check_vma=False)
```

```python
import math

import jax
import jax.numpy as jnp
from jax import lax
from jax.sharding import PartitionSpec as P

BLK = 8


def shift(x, axes, step):
    sizes = [lax.axis_size(a) for a in axes]
    pairs = []
    for src in range(math.prod(sizes)):
        coords, rest = [], src
        for size in reversed(sizes):
            coords.append(rest % size)
            rest //= size
        coords = coords[::-1]
        dst = [c + d for c, d in zip(coords, step)]
        if all(0 <= c < s for c, s in zip(dst, sizes)):
            flat = 0
            for c, s in zip(dst, sizes):
                flat = flat * s + c
            pairs.append((src, flat))
    return lax.ppermute(x, axes if len(axes) > 1 else axes[0], pairs)


def neighbour_pool(blocks, block_edge):
    e = block_edge
    n, s, v, c = blocks.shape
    rows = blocks.reshape(n, s, e, e * e, c)
    hi, lo = (e - 1) * e, e
    zero = jnp.zeros_like(rows)
    recv = {
        (-1, 0): zero.at[:, :, e - 1].set(shift(rows[:, :, e - 1], ("gx",), (1,))),
        (1, 0): zero.at[:, :, 0].set(shift(rows[:, :, 0], ("gx",), (-1,))),
        (0, -1): zero.at[:, :, :, hi:].set(shift(rows[:, :, :, hi:], ("gy",), (1,))),
        (0, 1): zero.at[:, :, :, :lo].set(shift(rows[:, :, :, :lo], ("gy",), (-1,))),
        (-1, -1): zero.at[:, :, e - 1, hi:].set(
            shift(rows[:, :, e - 1, hi:], ("gx", "gy"), (1, 1))
        ),
        (-1, 1): zero.at[:, :, e - 1, :lo].set(
            shift(rows[:, :, e - 1, :lo], ("gx", "gy"), (1, -1))
        ),
        (1, -1): zero.at[:, :, 0, hi:].set(shift(rows[:, :, 0, hi:], ("gx", "gy"), (-1, 1))),
        (1, 1): zero.at[:, :, 0, :lo].set(shift(rows[:, :, 0, :lo], ("gx", "gy"), (-1, -1))),
        (0, 0): rows,
    }
    pool = jnp.concatenate(
        [recv[(di, dj)] for di in (-1, 0, 1) for dj in (-1, 0, 1)], axis=1
    )
    return pool.reshape(n, 9 * s, v, c)


def padded_columns(pool, ids, slot_count, block_edge):
    e = block_edge
    c = pool.shape[-1]
    onehot = (ids[:, None] == jnp.arange(pool.shape[0])[None, :]).astype(pool.dtype)
    picked = jnp.einsum("mn,nvc->mvc", onehot, pool, preferred_element_type=jnp.float32)
    picked = picked.reshape(slot_count, 27, e, e, e, c)
    cube = assemble(picked, e)
    return im2col(cube, e).astype(pool.dtype)


def assemble(picked, block_edge):
    ranges = ((block_edge - 1, block_edge), (0, block_edge), (0, 1))
    planes = []
    for a in range(3):
        row_list = []
        for b in range(3):
            columns = []
            for c in range(3):
                k = (a * 3 + b) * 3 + c
                portion = picked[
                    :,
                    k,
                    ranges[a][0] : ranges[a][1],
                    ranges[b][0] : ranges[b][1],
                    ranges[c][0] : ranges[c][1],
                    :,
                ]
                columns.append(portion)
            row_list.append(jnp.concatenate(columns, axis=3))
        planes.append(jnp.concatenate(row_list, axis=2))
    return jnp.concatenate(planes, axis=1)


def im2col(cube, block_edge):
    windows = []
    for a in range(3):
        for b in range(3):
            for c in range(3):
                windows.append(
                    cube[:, a : a + block_edge, b : b + block_edge, c : c + block_edge, :]
                )
    cols = jnp.concatenate(windows, axis=-1)
    return cols.reshape(-1, cols.shape[-1])


def butterfly_sum(x, axes, later):
    n = math.prod(lax.axis_size(a) for a in axes)
    bits = n.bit_length() - 1
    flat = x.reshape(-1)
    me = lax.axis_index(axes)
    gx_bits = int(math.log2(lax.axis_size(axes[0])))
    gy_bits = bits - gx_bits
    order = [gy_bits + i for i in range(gx_bits)] + list(range(gy_bits))
    order = [order[0]] + sorted(order[1:], key=lambda b: (b % 3, b))
    pairs = lambda b: [(j, j ^ (1 << b)) for j in range(n)]
    for b in order:
        half = flat.shape[0] // 2
        bit = (me >> b) & 1
        keep = lax.dynamic_slice(flat, (bit * half,), (half,))
        send = lax.dynamic_slice(flat, ((1 - bit) * half,), (half,))
        flat = keep + lax.ppermute(send, axes, pairs(b))
        if later is not None:
            flat, later = lax.optimization_barrier((flat, later))
            held, later = later, None
    for b in reversed(order):
        bit = (me >> b) & 1
        other = lax.ppermute(flat, axes, pairs(b))
        flat = jnp.where(
            bit == 0, jnp.concatenate([flat, other]), jnp.concatenate([other, flat])
        )
    return flat.reshape(x.shape), held


def local(features, grad_out, weight, neighbours):
    slot_count = features.shape[2]
    voxels = features.shape[3]
    channels = features.shape[4]
    ids = neighbours.reshape(slot_count * 27)
    both = jnp.stack([features, grad_out]).reshape(2, slot_count, voxels, channels)
    pool = neighbour_pool(both, BLK)
    cols_feat = padded_columns(pool[0], ids, slot_count, BLK)
    grad_flat = grad_out.reshape(-1, channels)
    partial_value = lax.dot_general(
        cols_feat, grad_flat, (((0,), (0,)), ((), ())), preferred_element_type=jnp.float32
    ).reshape(27, channels, channels)
    summed, (pool_grad, cols_feat) = butterfly_sum(
        partial_value, ("gx", "gy"), (pool[1], cols_feat)
    )
    cols_grad = padded_columns(pool_grad, ids, slot_count, BLK)
    w_out = weight.reshape(27 * channels, channels)
    w_in = jnp.swapaxes(weight[::-1], 1, 2).reshape(27 * channels, channels)
    output = jnp.dot(cols_feat, w_out, preferred_element_type=jnp.float32)
    grad_in = jnp.dot(cols_grad, w_in, preferred_element_type=jnp.float32)
    total_slots = lax.axis_size("gx") * lax.axis_size("gy") * slot_count * voxels
    scale_factor = 1.0 / math.sqrt(total_slots)
    return (
        output.astype(jnp.bfloat16).reshape(features.shape),
        grad_in.astype(jnp.bfloat16).reshape(features.shape),
        summed * scale_factor,
    )


def solution(mesh):
    in_specs = (
        P("gx", "gy", None, None, None),
        P("gx", "gy", None, None, None),
        P(),
        P("gx", "gy", None, None),
    )
    out_specs = (P("gx", "gy", None, None, None), P("gx", "gy", None, None, None), P())
    return jax.shard_map(local, mesh=mesh, in_specs=in_specs, out_specs=out_specs, check_vma=False)
```

```python
import math

import jax
import jax.numpy as jnp
from jax import lax
from jax.sharding import PartitionSpec as P

BLK = 8


def shift(x, axes, step):
    sizes = [lax.axis_size(a) for a in axes]
    pairs = []
    for src in range(math.prod(sizes)):
        coords, rest = [], src
        for size in reversed(sizes):
            coords.append(rest % size)
            rest //= size
        coords = coords[::-1]
        dst = [c + d for c, d in zip(coords, step)]
        if all(0 <= c < s for c, s in zip(dst, sizes)):
            flat = 0
            for c, s in zip(dst, sizes):
                flat = flat * s + c
            pairs.append((src, flat))
    return lax.ppermute(x, axes if len(axes) > 1 else axes[0], pairs)


def neighbour_pool(blocks, block_edge):
    e = block_edge
    n, s, v, c = blocks.shape
    rows = blocks.reshape(n, s, e, e * e, c)
    hi, lo = (e - 1) * e, e
    zero = jnp.zeros_like(rows)
    from_ym = shift(rows[:, :, :, hi:], ("gy",), (1,))
    from_yp = shift(rows[:, :, :, :lo], ("gy",), (-1,))
    up = jnp.concatenate(
        [rows[:, :, e - 1], from_ym[:, :, e - 1], from_yp[:, :, e - 1]], axis=2
    )
    down = jnp.concatenate([rows[:, :, 0], from_ym[:, :, 0], from_yp[:, :, 0]], axis=2)
    from_xm = shift(up, ("gx",), (1,))
    from_xp = shift(down, ("gx",), (-1,))
    plane = e * e
    recv = {
        (-1, 0): zero.at[:, :, e - 1].set(from_xm[:, :, :plane]),
        (1, 0): zero.at[:, :, 0].set(from_xp[:, :, :plane]),
        (0, -1): zero.at[:, :, :, hi:].set(from_ym),
        (0, 1): zero.at[:, :, :, :lo].set(from_yp),
        (-1, -1): zero.at[:, :, e - 1, hi:].set(from_xm[:, :, plane : plane + e]),
        (-1, 1): zero.at[:, :, e - 1, :lo].set(from_xm[:, :, plane + e :]),
        (1, -1): zero.at[:, :, 0, hi:].set(from_xp[:, :, plane : plane + e]),
        (1, 1): zero.at[:, :, 0, :lo].set(from_xp[:, :, plane + e :]),
        (0, 0): rows,
    }
    pool = jnp.concatenate(
        [recv[(di, dj)] for di in (-1, 0, 1) for dj in (-1, 0, 1)], axis=1
    )
    return pool.reshape(n, 9 * s, v, c)


def padded_columns(pool, ids, slot_count, block_edge):
    e = block_edge
    c = pool.shape[-1]
    onehot = (ids[:, None] == jnp.arange(pool.shape[0])[None, :]).astype(pool.dtype)
    picked = jnp.einsum("mn,nvc->mvc", onehot, pool, preferred_element_type=jnp.float32)
    picked = picked.reshape(slot_count, 27, e, e, e, c)
    cube = assemble(picked, e)
    return im2col(cube, e).astype(pool.dtype)


def assemble(picked, block_edge):
    ranges = ((block_edge - 1, block_edge), (0, block_edge), (0, 1))
    planes = []
    for a in range(3):
        row_list = []
        for b in range(3):
            columns = []
            for c in range(3):
                k = (a * 3 + b) * 3 + c
                portion = picked[
                    :,
                    k,
                    ranges[a][0] : ranges[a][1],
                    ranges[b][0] : ranges[b][1],
                    ranges[c][0] : ranges[c][1],
                    :,
                ]
                columns.append(portion)
            row_list.append(jnp.concatenate(columns, axis=3))
        planes.append(jnp.concatenate(row_list, axis=2))
    return jnp.concatenate(planes, axis=1)


def im2col(cube, block_edge):
    windows = []
    for a in range(3):
        for b in range(3):
            for c in range(3):
                windows.append(
                    cube[:, a : a + block_edge, b : b + block_edge, c : c + block_edge, :]
                )
    cols = jnp.concatenate(windows, axis=-1)
    return cols.reshape(-1, cols.shape[-1])


def butterfly_sum(x, axes):
    n = math.prod(lax.axis_size(a) for a in axes)
    bits = n.bit_length() - 1
    flat = x.reshape(-1)
    me = lax.axis_index(axes)
    gx_bits = int(math.log2(lax.axis_size(axes[0])))
    gy_bits = bits - gx_bits
    order = [gy_bits + i for i in range(gx_bits)] + list(range(gy_bits))
    order = [order[0]] + sorted(order[1:], key=lambda b: (b % 3, b))
    pairs = lambda b: [(j, j ^ (1 << b)) for j in range(n)]
    for b in order:
        half = flat.shape[0] // 2
        bit = (me >> b) & 1
        keep = lax.dynamic_slice(flat, (bit * half,), (half,))
        send = lax.dynamic_slice(flat, ((1 - bit) * half,), (half,))
        flat = keep + lax.ppermute(send, axes, pairs(b))
    for b in reversed(order):
        bit = (me >> b) & 1
        other = lax.ppermute(flat, axes, pairs(b))
        flat = jnp.where(
            bit == 0, jnp.concatenate([flat, other]), jnp.concatenate([other, flat])
        )
    return flat.reshape(x.shape)


def local(features, grad_out, weight, neighbours):
    slot_count = features.shape[2]
    voxels = features.shape[3]
    channels = features.shape[4]
    ids = neighbours.reshape(slot_count * 27)
    both = jnp.stack([features, grad_out]).reshape(2, slot_count, voxels, channels)
    pool = neighbour_pool(both, BLK)
    cols_feat = padded_columns(pool[0], ids, slot_count, BLK)
    grad_flat = grad_out.reshape(-1, channels)
    partial_value = lax.dot_general(
        cols_feat, grad_flat, (((0,), (0,)), ((), ())), preferred_element_type=jnp.float32
    ).reshape(27, channels, channels)
    summed = butterfly_sum(partial_value, ("gx", "gy"))
    cols_grad = padded_columns(pool[1], ids, slot_count, BLK)
    w_out = weight.reshape(27 * channels, channels)
    w_in = jnp.swapaxes(weight[::-1], 1, 2).reshape(27 * channels, channels)
    output = jnp.dot(cols_feat, w_out, preferred_element_type=jnp.float32)
    grad_in = jnp.dot(cols_grad, w_in, preferred_element_type=jnp.float32)
    total_slots = lax.axis_size("gx") * lax.axis_size("gy") * slot_count * voxels
    scale_factor = 1.0 / math.sqrt(total_slots)
    return (
        output.astype(jnp.bfloat16).reshape(features.shape),
        grad_in.astype(jnp.bfloat16).reshape(features.shape),
        summed * scale_factor,
    )


def solution(mesh):
    in_specs = (
        P("gx", "gy", None, None, None),
        P("gx", "gy", None, None, None),
        P(),
        P("gx", "gy", None, None),
    )
    out_specs = (P("gx", "gy", None, None, None), P("gx", "gy", None, None, None), P())
    return jax.shard_map(local, mesh=mesh, in_specs=in_specs, out_specs=out_specs, check_vma=False)
```

```python
import math

import jax
import jax.numpy as jnp
from jax import lax
from jax.sharding import PartitionSpec as P


BLK = 8


def shift(x, axes, step):
    sizes = [lax.axis_size(a) for a in axes]
    pairs = []
    for src in range(math.prod(sizes)):
        coords, rest = [], src
        for size in reversed(sizes):
            coords.append(rest % size)
            rest //= size
        coords = coords[::-1]
        dst = [c + d for c, d in zip(coords, step)]
        if all(0 <= c < s for c, s in zip(dst, sizes)):
            flat = 0
            for c, s in zip(dst, sizes):
                flat = flat * s + c
            pairs.append((src, flat))
    return lax.ppermute(x, axes if len(axes) > 1 else axes[0], pairs)


def neighbour_pool(blocks, block_edge):
    e = block_edge
    n, s, v, c = blocks.shape
    rows = blocks.reshape(n, s, e, e * e, c)
    hi, lo = (e - 1) * e, e
    zero = jnp.zeros_like(rows)
    from_ym = shift(rows[:, :, :, hi:], ("gy",), (1,))
    from_yp = shift(rows[:, :, :, :lo], ("gy",), (-1,))
    up = jnp.concatenate(
        [rows[:, :, e - 1], from_ym[:, :, e - 1], from_yp[:, :, e - 1]], axis=2
    )
    down = jnp.concatenate([rows[:, :, 0], from_ym[:, :, 0], from_yp[:, :, 0]], axis=2)
    from_xm = shift(up, ("gx",), (1,))
    from_xp = shift(down, ("gx",), (-1,))
    plane = e * e
    recv = {
        (-1, 0): zero.at[:, :, e - 1].set(from_xm[:, :, :plane]),
        (1, 0): zero.at[:, :, 0].set(from_xp[:, :, :plane]),
        (0, -1): zero.at[:, :, :, hi:].set(from_ym),
        (0, 1): zero.at[:, :, :, :lo].set(from_yp),
        (-1, -1): zero.at[:, :, e - 1, hi:].set(from_xm[:, :, plane : plane + e]),
        (-1, 1): zero.at[:, :, e - 1, :lo].set(from_xm[:, :, plane + e :]),
        (1, -1): zero.at[:, :, 0, hi:].set(from_xp[:, :, plane : plane + e]),
        (1, 1): zero.at[:, :, 0, :lo].set(from_xp[:, :, plane + e :]),
        (0, 0): rows,
    }
    pool = jnp.concatenate(
        [recv[(di, dj)] for di in (-1, 0, 1) for dj in (-1, 0, 1)], axis=1
    )
    return pool.reshape(n, 9 * s, v, c)


def padded_columns(pool, ids, slot_count, block_edge):
    e = block_edge
    c = pool.shape[-1]
    onehot = (ids[:, None] == jnp.arange(pool.shape[0])[None, :]).astype(pool.dtype)
    picked = jnp.einsum("mn,nvc->mvc", onehot, pool, preferred_element_type=jnp.float32)
    picked = picked.reshape(slot_count, 27, e, e, e, c)
    cube = assemble(picked, e)
    return im2col(cube, e).astype(pool.dtype)


def assemble(picked, block_edge):
    ranges = ((block_edge - 1, block_edge), (0, block_edge), (0, 1))
    planes = []
    for a in range(3):
        row_list = []
        for b in range(3):
            columns = []
            for c in range(3):
                k = (a * 3 + b) * 3 + c
                portion = picked[
                    :,
                    k,
                    ranges[a][0] : ranges[a][1],
                    ranges[b][0] : ranges[b][1],
                    ranges[c][0] : ranges[c][1],
                    :,
                ]
                columns.append(portion)
            row_list.append(jnp.concatenate(columns, axis=3))
        planes.append(jnp.concatenate(row_list, axis=2))
    return jnp.concatenate(planes, axis=1)


def im2col(cube, block_edge):
    windows = []
    for a in range(3):
        for b in range(3):
            for c in range(3):
                windows.append(
                    cube[:, a : a + block_edge, b : b + block_edge, c : c + block_edge, :]
                )
    cols = jnp.concatenate(windows, axis=-1)
    return cols.reshape(-1, cols.shape[-1])


def butterfly_sum(x, axes):
    n = math.prod(lax.axis_size(a) for a in axes)
    bits = n.bit_length() - 1
    flat = x.reshape(-1)
    me = lax.axis_index(axes)
    gx_bits = int(math.log2(lax.axis_size(axes[0])))
    gy_bits = bits - gx_bits
    order = [gy_bits + i for i in range(gx_bits)] + list(range(gy_bits))
    order = [order[0]] + sorted(order[1:], key=lambda b: (b % 3, b))
    pairs = lambda b: [(j, j ^ (1 << b)) for j in range(n)]
    for b in order:
        half = flat.shape[0] // 2
        bit = (me >> b) & 1
        keep = lax.dynamic_slice(flat, (bit * half,), (half,))
        send = lax.dynamic_slice(flat, ((1 - bit) * half,), (half,))
        got = lax.ppermute(send, axes, pairs(b))
        flat = keep + got
    for b in reversed(order):
        bit = (me >> b) & 1
        other = lax.ppermute(flat, axes, pairs(b))
        flat = jnp.where(
            bit == 0, jnp.concatenate([flat, other]), jnp.concatenate([other, flat])
        )
    return flat.reshape(x.shape)


def local_body(features, grad_out, weight, neighbours):
    slot_count = features.shape[2]
    voxels = features.shape[3]
    channels = features.shape[4]
    ids = neighbours.reshape(slot_count * 27)
    both = jnp.stack([features, grad_out]).reshape(2, slot_count, voxels, channels)
    pool = neighbour_pool(both, BLK)
    cols_feat = padded_columns(pool[0], ids, slot_count, BLK)
    grad_flat = grad_out.reshape(-1, channels)
    partial_value = lax.dot_general(
        cols_feat, grad_flat, (((0,), (0,)), ((), ())), preferred_element_type=jnp.float32
    ).reshape(27, channels, channels)
    summed = butterfly_sum(partial_value, ("gx", "gy"))
    cols_grad = padded_columns(pool[1], ids, slot_count, BLK)
    w_out = weight.reshape(27 * channels, channels)
    w_in = jnp.swapaxes(weight[::-1], 1, 2).reshape(27 * channels, channels)
    output = jnp.dot(cols_feat, w_out, preferred_element_type=jnp.float32)
    grad_in = jnp.dot(cols_grad, w_in, preferred_element_type=jnp.float32)
    total_slots = lax.axis_size("gx") * lax.axis_size("gy") * slot_count * voxels
    scale_factor = 1.0 / math.sqrt(total_slots)
    return (
        output.astype(jnp.bfloat16).reshape(features.shape),
        grad_in.astype(jnp.bfloat16).reshape(features.shape),
        summed * scale_factor,
    )


def solution(mesh):
    in_specs = (
        P("gx", "gy", None, None, None),
        P("gx", "gy", None, None, None),
        P(),
        P("gx", "gy", None, None),
    )
    out_specs = (P("gx", "gy", None, None, None), P("gx", "gy", None, None, None), P())
    return jax.shard_map(local_body, mesh=mesh, in_specs=in_specs, out_specs=out_specs, check_vma=False)
```
